32 devices in a mesh: seq: 8 (over z, y), fsdp: 4 (over x, core).
Axes of the slice: x: 2, y: 2, z: 4, core: 2. Of those that a mesh axis runs over, the one named last changes fastest.
Arguments:
- tokens: bfloat16 [4, 1024, 768], P('fsdp', 'seq')
- lengths: int32 [4], P('fsdp'), may hold values from 341 to 1024
- block_order: int32 [8], replicated, may hold values from 0 to 7, each once
- qkv_weight: bfloat16 [768, 2304], P('fsdp'), may hold values from -0.21875 to 0.21875
- q_bias: bfloat16 [768], P('fsdp'), may hold values from -3 to 3
- v_bias: bfloat16 [768], P('fsdp'), may hold values from -0.119628906 to 0.119628906
- out_weight: bfloat16 [768, 768], P('fsdp'), may hold values from -6 to 6
- out_bias: bfloat16 [768], P('fsdp'), may hold values from -3 to 3
- norm1_gain: bfloat16 [768], P('fsdp'), may hold values from 0.5 to 1.5
- norm1_shift: bfloat16 [768], P('fsdp'), may hold values from -3 to 3
- up_weight: bfloat16 [768, 3072], P('fsdp'), may hold values from -0.21875 to 0.21875
- up_bias: bfloat16 [3072], P('fsdp'), may hold values from -3 to 3
- down_weight: bfloat16 [3072, 768], P('fsdp'), may hold values from -0.109375 to 0.109375
- down_bias: bfloat16 [768], P('fsdp'), may hold values from -3 to 3
- norm2_gain: bfloat16 [768], P('fsdp'), may hold values from 0.5 to 1.5
- norm2_shift: bfloat16 [768], P('fsdp'), may hold values from -3 to 3
- cotangent: bfloat16 [4, 1024, 768], P('fsdp', 'seq'), may hold values from -6 to 6
Outputs:
- encoded: bfloat16 [4, 1024, 768], P('fsdp', 'seq')
- input_grad: float32 [4, 1024, 768], P('fsdp', 'seq')
- qkv_grad: float32 [768, 2304], P('fsdp')
- q_bias_grad: float32 [768], P('fsdp')
- v_bias_grad: float32 [768], P('fsdp')
- out_weight_grad: float32 [768, 768], P('fsdp')
- out_bias_grad: float32 [768], P('fsdp')
- norm1_gain_grad: float32 [768], P('fsdp')
- norm1_shift_grad: float32 [768], P('fsdp')
- up_weight_grad: float32 [768, 3072], P('fsdp')
- up_bias_grad: float32 [3072], P('fsdp')
- down_weight_grad: float32 [3072, 768], P('fsdp')
- down_bias_grad: float32 [768], P('fsdp')
- norm2_gain_grad: float32 [768], P('fsdp')
- norm2_shift_grad: float32 [768], P('fsdp')
The draws below stay inside these ranges and needn't reach their ends.
Inputs may be any that keep to these rules, and one draw needn't show every extreme that they name: Rows j * 128 to (j + 1) * 128 - 1 of each sequence in tokens and cotangent hold the positions block_order[j] * 128 onward; each block number appears once. The first lengths[s] positions of sequence s are real tokens; only they serve as keys.
All inputs are finite; a program needn't handle non-finite values.
Results may differ from the reference program's by a relative error of at most 0.018.
The reference program's roundings to bfloat16 on the way (of `context`, `activated`, `grad_context` and `mixed`) count: a program that leaves them out, or rounds other values in their place, can miss the bound.
Values may be sent and summed in bfloat16 or wider, within the bound.
No kernel may reach another device: no remote copies, remote signals or barrier semaphores. Data moves between devices by JAX's collectives and lax.ppermute only.
A program may use at most 192 MiB of HBM per device.

```python
import jax
import jax.numpy as jnp
from jax import lax

D = 768
HEADS = 12
HDIM = 64
FF = 3072
LEN = 1024
SEQS = 4
TOKENS = 4096
N_SEQ = 8


def draw_tokens(key, part):
    first_key = jax.random.fold_in(key, 0)
    normal_part = jnp.clip(jax.random.normal(first_key, (SEQS, LEN, D), jnp.float32), -6.0, 6.0)
    return normal_part.astype(jnp.bfloat16)


def set_ends(drawn, rng, least, top_value):
    longest = drawn.shape.index(max(drawn.shape))
    spots = []
    for shift in (0, 1):
        where = [jax.random.randint(jax.random.fold_in(rng, axis), (), 0, length) for axis, length in enumerate(drawn.shape)]
        where[longest] = (where[longest] + shift) % drawn.shape[longest]
        spots.append(tuple(where))
    return drawn.at[spots[0]].set(least).at[spots[1]].set(top_value)


def shard_levels(stream_key, shape, pieces, low, high):
    def one(position, shards_of):
        heights = jax.random.uniform(jax.random.fold_in(jax.random.fold_in(stream_key, 6), position), (shards_of,), jnp.float32, low / len(pieces), high / len(pieces))
        return jnp.repeat(jnp.exp(heights), shape[position] // shards_of).reshape((-1,) + (1,) * (len(shape) - position - 1))

    loudness = one(*pieces[0])
    for cut in pieces[1:]:
        loudness = loudness * one(*cut)
    return loudness


def centred(key, dims, scale, limit, pieces=(), kind=jnp.bfloat16):
    array = scale * jax.random.normal(key, dims, jnp.float32)
    if pieces:
        array = array * shard_levels(key, dims, pieces, -0.22, 0.18)
    return jnp.clip(array, -limit, limit).astype(kind)


def setup_inputs(seed: int = 0) -> dict:
    splits = jax.random.split(jax.random.key(seed), 18)
    tokens = draw_tokens(jax.random.fold_in(splits[17], 71), 0)
    lengths = set_ends(jax.random.randint(splits[1], (SEQS,), LEN // 3, LEN + 1), jax.random.fold_in(splits[1], 1), LEN // 3, LEN).astype(jnp.int32)
    block_order = jax.random.permutation(splits[2], N_SEQ).astype(jnp.int32)
    qkv_weight = centred(splits[3], (D, 3 * D), D ** -0.5, 0.21875, ((0, 4),))
    q_bias = centred(splits[4], (D,), 0.5, 3.0, ((0, 4),))
    v_bias = centred(splits[5], (D,), 0.02, 0.119628906, ((0, 4),))
    out_weight = centred(splits[6], (D, D), 1.0, 6.0, ((0, 4),))
    out_bias = centred(splits[7], (D,), 0.5, 3.0, ((0, 4),))
    norm1_gain = jnp.clip(1.0 + 0.1 * jax.random.normal(splits[8], (D,), jnp.float32), 0.5, 1.5).astype(jnp.bfloat16)
    norm1_shift = centred(splits[9], (D,), 0.5, 3.0, ((0, 4),))
    up_weight = centred(splits[10], (D, FF), D ** -0.5, 0.21875, ((0, 4),))
    up_bias = centred(splits[11], (FF,), 0.5, 3.0, ((0, 4),))
    down_weight = centred(splits[12], (FF, D), FF ** -0.5, 0.109375, ((0, 4),))
    down_bias = centred(splits[13], (D,), 0.5, 3.0, ((0, 4),))
    norm2_gain = jnp.clip(1.0 + 0.1 * jax.random.normal(splits[14], (D,), jnp.float32), 0.5, 1.5).astype(jnp.bfloat16)
    norm2_shift = centred(splits[15], (D,), 0.5, 3.0, ((0, 4),))
    cotangent = centred(splits[16], (SEQS, LEN, D), 1.0, 6.0, ((0, 4), (1, 8)))
    return {"tokens": tokens, "lengths": lengths, "block_order": block_order, "qkv_weight": qkv_weight, "q_bias": q_bias, "v_bias": v_bias, "out_weight": out_weight, "out_bias": out_bias, "norm1_gain": norm1_gain, "norm1_shift": norm1_shift, "up_weight": up_weight, "up_bias": up_bias, "down_weight": down_weight, "down_bias": down_bias, "norm2_gain": norm2_gain, "norm2_shift": norm2_shift, "cotangent": cotangent}


epsilon = 1e-06
masked_out = -1e+30

def rounded(value):
    return lax.optimization_barrier(value.astype(jnp.bfloat16)).astype(jnp.float32)

def positions(block_order, block_len):
    offsets = jnp.arange(block_len, dtype=jnp.int32)
    return (block_order.astype(jnp.int32)[:, None] * block_len + offsets[None, :]).reshape(-1)

def norm_forward(hidden, gain, shift):
    centre = hidden - lax.optimization_barrier(jnp.mean(hidden, axis=-1, keepdims=True))
    spread = lax.rsqrt(lax.optimization_barrier(jnp.mean(centre * centre, axis=-1, keepdims=True)) + epsilon)
    normed = centre * spread
    return (normed * gain + shift, normed, spread)

def norm_backward(upstream, normed, spread, gain):
    scaled = upstream * gain
    grad_in = spread * (scaled - lax.optimization_barrier(jnp.mean(scaled, axis=-1, keepdims=True)) - normed * lax.optimization_barrier(jnp.mean(scaled * normed, axis=-1, keepdims=True)))
    return (grad_in, lax.optimization_barrier(jnp.sum(upstream * normed, axis=0)), lax.optimization_barrier(jnp.sum(upstream, axis=0)))

def gelu_exact(pre):
    return 0.5 * pre * (1.0 + lax.erf(pre * 0.7071067811865476))

def gelu_slope(pre):
    return 0.5 * (1.0 + lax.erf(pre * 0.7071067811865476)) + pre * jnp.exp(-0.5 * pre * pre) * 0.3989422804014327

def reference(tokens, lengths, block_order, qkv_weight, q_bias, v_bias, out_weight, out_bias, norm1_gain, norm1_shift, up_weight, up_bias, down_weight, down_bias, norm2_gain, norm2_shift, cotangent):
    block_len = LEN // N_SEQ
    key_pos = positions(block_order, block_len)
    query_block = min(512, LEN)
    query_steps = LEN // query_block
    score_scale = HDIM ** (-0.5)
    bias_q = q_bias.astype(jnp.float32)
    bias_v = v_bias.astype(jnp.float32)
    bias_out = out_bias.astype(jnp.float32)
    gain_one = norm1_gain.astype(jnp.float32)
    shift_one = norm1_shift.astype(jnp.float32)
    bias_up = up_bias.astype(jnp.float32)
    bias_down = down_bias.astype(jnp.float32)
    gain_two = norm2_gain.astype(jnp.float32)
    shift_two = norm2_shift.astype(jnp.float32)
    head_shape = (LEN, HEADS, HDIM)
    block_shape = (query_steps, query_block, HEADS, HDIM)

    def one_sequence(carry, inputs):
        seq_tokens, seq_cot, seq_len = inputs
        valid = key_pos < seq_len
        projected = jnp.dot(seq_tokens, qkv_weight, preferred_element_type=jnp.float32)
        queries = rounded(projected[:, :D] + bias_q).reshape(head_shape)
        keys_f = rounded(projected[:, D:2 * D]).reshape(head_shape)
        values_f = rounded(projected[:, 2 * D:] + bias_v).reshape(head_shape)

        def logits_for(query_rows):
            logits = jnp.einsum('qhd,khd->hqk', query_rows, keys_f) * score_scale
            return jnp.where(valid[None, None, :], logits, masked_out)

        def attend(query_rows):
            logits = logits_for(query_rows)
            top = lax.optimization_barrier(jnp.max(logits, axis=-1, keepdims=True))
            total = lax.optimization_barrier(jnp.sum(jnp.where(valid[None, None, :], jnp.exp(logits - top), 0.0), axis=-1, keepdims=True))
            log_total = top + jnp.log(total)
            probs = rounded(jnp.where(valid[None, None, :], jnp.exp(logits - log_total), 0.0))
            context = jnp.einsum('hqk,khd->qhd', probs, values_f)
            return (context.astype(jnp.bfloat16), log_total[..., 0])
        context, log_total = lax.map(attend, queries.reshape(block_shape))
        context = context.reshape(LEN, D)
        attended = jnp.dot(context, out_weight, preferred_element_type=jnp.float32) + bias_out
        first_sum = seq_tokens.astype(jnp.float32) + attended
        first_out, first_norm, first_spread = norm_forward(first_sum, gain_one, shift_one)
        first_bf = first_out.astype(jnp.bfloat16)
        pre_act = jnp.dot(first_bf, up_weight, preferred_element_type=jnp.float32) + bias_up
        activated = gelu_exact(pre_act).astype(jnp.bfloat16)
        second_sum = first_out + jnp.dot(activated, down_weight, preferred_element_type=jnp.float32) + bias_down
        second_out, second_norm, second_spread = norm_forward(second_sum, gain_two, shift_two)
        encoded = second_out.astype(jnp.bfloat16)
        upstream = seq_cot.astype(jnp.float32)
        grad_second, grad_gain_two, grad_shift_two = norm_backward(upstream, second_norm, second_spread, gain_two)
        grad_second_bf = grad_second.astype(jnp.bfloat16)
        grad_act = jnp.dot(grad_second_bf, down_weight.T, preferred_element_type=jnp.float32)
        grad_pre = grad_act * gelu_slope(pre_act)
        grad_pre_bf = grad_pre.astype(jnp.bfloat16)
        grad_first_out = grad_second + jnp.dot(grad_pre_bf, up_weight.T, preferred_element_type=jnp.float32)
        grad_first, grad_gain_one, grad_shift_one = norm_backward(grad_first_out, first_norm, first_spread, gain_one)
        grad_first_bf = grad_first.astype(jnp.bfloat16)
        grad_context = rounded(jnp.dot(grad_first_bf, out_weight.T, preferred_element_type=jnp.float32)).reshape(head_shape)
        context_f = context.astype(jnp.float32).reshape(head_shape)
        correction = lax.optimization_barrier(jnp.sum(grad_context * context_f, axis=-1))
        corr_blocks = correction.reshape(query_steps, query_block, HEADS).transpose(0, 2, 1)

        def backward_block(state, blocks):
            grad_keys, grad_values = state
            query_rows, grad_rows, lse_rows, corr_rows = blocks
            logits = logits_for(query_rows)
            probs = jnp.where(valid[None, None, :], jnp.exp(logits - lse_rows[..., None]), 0.0)
            grad_logit = jnp.einsum('qhd,khd->hqk', grad_rows, values_f)
            mixed = rounded(probs * (grad_logit - corr_rows[..., None]))
            grad_query = jnp.einsum('hqk,khd->qhd', mixed, keys_f) * score_scale
            grad_keys = grad_keys + jnp.einsum('hqk,qhd->khd', mixed, query_rows) * score_scale
            grad_values = grad_values + jnp.einsum('hqk,qhd->khd', rounded(probs), grad_rows)
            return ((grad_keys, grad_values), grad_query)
        zero_heads = jnp.zeros(head_shape, jnp.float32)
        (grad_keys, grad_values), grad_query = lax.scan(backward_block, (zero_heads, zero_heads), (queries.reshape(block_shape), grad_context.reshape(block_shape), log_total, corr_blocks))
        grad_query = grad_query.reshape(LEN, D)
        grad_keys = grad_keys.reshape(LEN, D)
        grad_values = grad_values.reshape(LEN, D)
        grad_qkv_bf = jnp.concatenate([grad_query.astype(jnp.bfloat16), grad_keys.astype(jnp.bfloat16), grad_values.astype(jnp.bfloat16)], axis=1)
        input_grad = grad_first + jnp.dot(grad_qkv_bf, qkv_weight.T, preferred_element_type=jnp.float32)
        terms = (jnp.dot(seq_tokens.T, grad_qkv_bf, preferred_element_type=jnp.float32), lax.optimization_barrier(jnp.sum(grad_query, axis=0)), lax.optimization_barrier(jnp.sum(grad_values, axis=0)), jnp.dot(context.T, grad_first_bf, preferred_element_type=jnp.float32), lax.optimization_barrier(jnp.sum(grad_first, axis=0)), grad_gain_one, grad_shift_one, jnp.dot(first_bf.T, grad_pre_bf, preferred_element_type=jnp.float32), lax.optimization_barrier(jnp.sum(grad_pre, axis=0)), jnp.dot(activated.T, grad_second_bf, preferred_element_type=jnp.float32), lax.optimization_barrier(jnp.sum(grad_second, axis=0)), grad_gain_two, grad_shift_two)
        updated = jax.tree.map(lambda total, item: total + item, carry, terms)
        return (updated, (encoded, input_grad))
    start = (jnp.zeros((D, 3 * D), jnp.float32), jnp.zeros((D,), jnp.float32), jnp.zeros((D,), jnp.float32), jnp.zeros((D, D), jnp.float32), jnp.zeros((D,), jnp.float32), jnp.zeros((D,), jnp.float32), jnp.zeros((D,), jnp.float32), jnp.zeros((D, FF), jnp.float32), jnp.zeros((FF,), jnp.float32), jnp.zeros((FF, D), jnp.float32), jnp.zeros((D,), jnp.float32), jnp.zeros((D,), jnp.float32), jnp.zeros((D,), jnp.float32))
    grads, (encoded, input_grad) = lax.scan(one_sequence, start, (tokens, cotangent, lengths))
    factor = TOKENS ** (-0.5)
    return (encoded, input_grad, grads[0] * factor, grads[1] * factor, grads[2] * factor, grads[3] * factor, grads[4] * factor, grads[5] * factor, grads[6] * factor, grads[7] * factor, grads[8] * factor, grads[9] * factor, grads[10] * factor, grads[11] * factor, grads[12] * factor)
```

```python
import functools

import jax
import jax.numpy as jnp
from jax import lax
from jax.experimental import pallas as pl
from jax.experimental.pallas import tpu as pltpu
from jax.sharding import PartitionSpec as P

HEADS = 12

epsilon = 1e-06
masked_out = -1e30
bf16 = jnp.bfloat16
f32 = jnp.float32


def norm_forward(hidden, gain, shift):
    centre = hidden - jnp.mean(hidden, axis=-1, keepdims=True)
    spread = lax.rsqrt(jnp.mean(centre * centre, axis=-1, keepdims=True) + epsilon)
    normed = centre * spread
    return (normed * gain + shift, normed, spread)


def norm_backward(upstream, normed, spread, gain):
    scaled = upstream * gain
    grad_in = spread * (
        scaled
        - jnp.mean(scaled, axis=-1, keepdims=True)
        - normed * jnp.mean(scaled * normed, axis=-1, keepdims=True)
    )
    return (grad_in, jnp.sum(upstream * normed, axis=0), jnp.sum(upstream, axis=0))


def gelu_exact(pre):
    return 0.5 * pre * (1.0 + lax.erf(pre * 0.7071067811865476))


def gelu_slope(pre):
    return (
        0.5 * (1.0 + lax.erf(pre * 0.7071067811865476))
        + pre * jnp.exp(-0.5 * pre * pre) * 0.3989422804014327
    )


def swap(value, axis, mask):
    count = lax.axis_size(axis)
    return lax.ppermute(value, axis, [(i, i ^ mask) for i in range(count)])


def masks_of(count):
    found = []
    bit = count // 2
    while bit:
        found.append(bit)
        bit //= 2
    return found


def relative_order(count):
    order = [0]
    for mask in masks_of(count):
        order = order + [item ^ mask for item in order]
    return order


def gather_rows(value, axis):
    for mask in masks_of(lax.axis_size(axis)):
        value = jnp.concatenate([value, swap(value, axis, mask)], axis=0)
    return value


def scatter_rows(partial, axis):
    for mask in reversed(masks_of(lax.axis_size(axis))):
        half = partial.shape[0] // 2
        sent = swap(partial[half:].astype(bf16), axis, mask)
        partial = partial[:half].astype(f32) + sent.astype(f32)
    return partial


def pick(stack, index):
    return lax.dynamic_index_in_dim(stack, index, 0, keepdims=False)


def reorder(stack, base):
    return jnp.stack([pick(stack, base ^ g) for g in range(stack.shape[0])])


def exchange(stack, axis, base, stride, count):
    return [pick(stack, base)] + [
        swap(pick(stack, base ^ m), axis, m * stride) for m in range(1, count)
    ]


def attend_kernel(heads, size, scale, q_ref, k_ref, v_ref, bias_ref, ctx_ref, lse_ref):
    bias = bias_ref[...]
    lanes = lax.broadcasted_iota(jnp.int32, lse_ref.shape, 1)
    stats = jnp.zeros(lse_ref.shape, f32)
    outs = []
    for h in range(heads):
        cols = slice(h * size, (h + 1) * size)
        logits = (
            lax.dot_general(
                q_ref[:, cols], k_ref[:, cols], (((1,), (1,)), ((), ())), preferred_element_type=f32
            )
            * scale
            + bias
        )
        top = jnp.max(logits, axis=-1, keepdims=True)
        terms = jnp.exp(logits - top)
        total = jnp.sum(terms, axis=-1, keepdims=True)
        context = jnp.dot(terms.astype(bf16), v_ref[:, cols], preferred_element_type=f32)
        outs.append(context / total)
        stats = jnp.where(lanes == h, top + jnp.log(total), stats)
    ctx_ref[...] = jnp.concatenate(outs, axis=1).astype(bf16)
    lse_ref[...] = stats


def attend(queries, keys, values, bias, heads):
    rows, width = queries.shape
    full_len = keys.shape[0]
    size = width // heads
    tile = min(128, rows)
    whole = lambda i: (0, 0)
    return pl.pallas_call(
        functools.partial(attend_kernel, heads, size, size ** (-0.5)),
        grid=(rows // tile,),
        in_specs=[
            pl.BlockSpec((tile, width), lambda i: (i, 0)),
            pl.BlockSpec((full_len, width), whole),
            pl.BlockSpec((full_len, width), whole),
            pl.BlockSpec((1, full_len), whole),
        ],
        out_specs=[
            pl.BlockSpec((tile, width), lambda i: (i, 0)),
            pl.BlockSpec((tile, 128), lambda i: (i, 0)),
        ],
        out_shape=[
            jax.ShapeDtypeStruct((rows, width), bf16),
            jax.ShapeDtypeStruct((rows, 128), f32),
        ],
        cost_estimate=pl.CostEstimate(
            flops=4 * rows * full_len * width,
            bytes_accessed=4 * (rows + full_len) * width,
            transcendentals=rows * full_len * heads,
        ),
        name="attend",
    )(queries, keys, values, bias)


def attend_back_kernel(
    heads, size, scale, q_ref, k_ref, v_ref, bias_ref, lse_ref, ctx_ref, g_ref, dq_ref, dk_ref, dv_ref
):
    @pl.when(pl.program_id(0) == 0)
    def _():
        dk_ref[...] = jnp.zeros_like(dk_ref)
        dv_ref[...] = jnp.zeros_like(dv_ref)

    bias = bias_ref[...]
    dqs, dks, dvs = [], [], []
    for h in range(heads):
        cols = slice(h * size, (h + 1) * size)
        q_h, k_h, v_h, g_h = q_ref[:, cols], k_ref[:, cols], v_ref[:, cols], g_ref[:, cols]
        logits = (
            lax.dot_general(q_h, k_h, (((1,), (1,)), ((), ())), preferred_element_type=f32) * scale
            + bias
        )
        probs = jnp.exp(logits - lse_ref[:, h : h + 1])
        grad_logit = lax.dot_general(
            g_h, v_h, (((1,), (1,)), ((), ())), preferred_element_type=f32
        )
        correction = jnp.sum(
            g_h.astype(f32) * ctx_ref[:, cols].astype(f32), axis=-1, keepdims=True
        )
        mixed = (probs * (grad_logit - correction)).astype(bf16)
        dqs.append(jnp.dot(mixed, k_h, preferred_element_type=f32) * scale)
        dks.append(
            lax.dot_general(mixed, q_h, (((0,), (0,)), ((), ())), preferred_element_type=f32)
            * scale
        )
        dvs.append(
            lax.dot_general(
                probs.astype(bf16), g_h, (((0,), (0,)), ((), ())), preferred_element_type=f32
            )
        )
    dq_ref[...] = jnp.concatenate(dqs, axis=1)
    dk_ref[...] += jnp.concatenate(dks, axis=1)
    dv_ref[...] += jnp.concatenate(dvs, axis=1)


def attend_back(queries, keys, values, bias, lse, context, grad, heads):
    rows, width = queries.shape
    full_len = keys.shape[0]
    size = width // heads
    tile = min(128, rows)
    whole = lambda i: (0, 0)
    part = lambda i: (i, 0)
    return pl.pallas_call(
        functools.partial(attend_back_kernel, heads, size, size ** (-0.5)),
        grid=(rows // tile,),
        in_specs=[
            pl.BlockSpec((tile, width), part),
            pl.BlockSpec((full_len, width), whole),
            pl.BlockSpec((full_len, width), whole),
            pl.BlockSpec((1, full_len), whole),
            pl.BlockSpec((tile, 128), part),
            pl.BlockSpec((tile, width), part),
            pl.BlockSpec((tile, width), part),
        ],
        out_specs=[
            pl.BlockSpec((tile, width), part),
            pl.BlockSpec((full_len, width), whole),
            pl.BlockSpec((full_len, width), whole),
        ],
        out_shape=[
            jax.ShapeDtypeStruct((rows, width), f32),
            jax.ShapeDtypeStruct((full_len, width), f32),
            jax.ShapeDtypeStruct((full_len, width), f32),
        ],
        cost_estimate=pl.CostEstimate(
            flops=10 * rows * full_len * width,
            bytes_accessed=8 * (rows + full_len) * width,
            transcendentals=rows * full_len * heads,
        ),
        name="attend_back",
    )(queries, keys, values, bias, lse, context, grad)


def dot(a, b):
    return jnp.dot(a, b, preferred_element_type=f32)


def dot_nt(a, b):
    return lax.dot_general(a, b, (((1,), (1,)), ((), ())), preferred_element_type=f32)


def dot_tn(a, b):
    return lax.dot_general(a, b, (((0,), (0,)), ((), ())), preferred_element_type=f32)


def halve_sum(chunks, axis):
    me = lax.axis_index(axis)
    for level, mask in enumerate(reversed(masks_of(lax.axis_size(axis)))):
        bit = (me >> level) & 1
        paired = chunks.reshape((chunks.shape[0] // 2, 2) + chunks.shape[1:])
        kept = lax.dynamic_index_in_dim(paired, bit, 1, keepdims=False)
        sent = lax.dynamic_index_in_dim(paired, 1 - bit, 1, keepdims=False)
        chunks = (kept.astype(f32) + swap(sent, axis, mask).astype(f32)).astype(bf16)
    return chunks[0]


def double_gather(chunk, axis):
    me = lax.axis_index(axis)
    masks = masks_of(lax.axis_size(axis))
    chunks = chunk[None, None]
    for level, mask in zip(reversed(range(len(masks))), masks):
        bit = (me >> level) & 1
        other = swap(chunks, axis, mask)
        low = jnp.where(bit == 0, chunks, other)
        high = jnp.where(bit == 0, other, chunks)
        chunks = jnp.concatenate([low, high], axis=1)
        chunks = chunks.reshape((chunks.shape[0] * 1,) + chunks.shape[1:])
        chunks = chunks.reshape((chunks.shape[0] * chunks.shape[1], 1) + chunks.shape[2:])
    return chunks[:, 0]


def sum_small(value, axes):
    for axis in axes:
        for mask in masks_of(lax.axis_size(axis)):
            value = value + swap(value, axis, mask)
    return value


def body(
    tokens,
    lengths,
    block_order,
    qkv_weight,
    q_bias,
    v_bias,
    out_weight,
    out_bias,
    norm1_gain,
    norm1_shift,
    up_weight,
    up_bias,
    down_weight,
    down_bias,
    norm2_gain,
    norm2_shift,
    cotangent,
):
    seq_local, block_len, model_width = tokens.shape
    seq_count = lax.axis_size("seq")
    fsdp_count = lax.axis_size("fsdp")
    me_f = lax.axis_index("fsdp")
    me_s = lax.axis_index("seq")
    stride = seq_count // fsdp_count
    zone = me_s // stride
    lane = me_s % stride
    part_width = model_width // fsdp_count
    heads_own = HEADS // fsdp_count
    grad_scale = (block_len * seq_local * seq_count * fsdp_count) ** (-0.5)
    order = relative_order(fsdp_count)

    def columns(weight, pieces):
        rows, total = weight.shape
        split = weight.reshape(rows, pieces, fsdp_count, total // (pieces * fsdp_count))
        split = jnp.moveaxis(split, 2, 0).reshape(fsdp_count, rows, total // fsdp_count)
        return exchange(split, "fsdp", me_f, 1, fsdp_count)

    flat_in = tokens.reshape(block_len, model_width)
    all_in = gather_rows(flat_in, "fsdp")
    qkv_own = reorder(jnp.stack(columns(qkv_weight, 3)), me_f).reshape(model_width, 3 * part_width)

    vectors = jnp.stack(
        [item.astype(f32) for item in (out_bias, norm1_gain, norm1_shift, down_bias, norm2_gain, norm2_shift)]
        + [jnp.broadcast_to(lengths.astype(f32), (part_width,))]
    )
    vectors = gather_rows(vectors[None], "fsdp")
    length = pick(vectors, zone)[-1, 0].astype(jnp.int32)
    inverse = [order.index(r) for r in range(fsdp_count)]
    by_relative = jnp.stack([vectors[inverse[r]] for r in range(fsdp_count)])
    full = jnp.moveaxis(reorder(by_relative, me_f), 0, 1).reshape(-1, model_width)
    bias_out, gain_one, shift_one, bias_down, gain_two, shift_two = [full[i] for i in range(6)]

    projected = dot(all_in, qkv_own)
    added = jnp.concatenate(
        [q_bias.astype(f32), jnp.zeros((part_width,), f32), v_bias.astype(f32)]
    )
    qkv = (projected + added).astype(bf16).reshape(fsdp_count, block_len, 3 * part_width)
    arrived = exchange(qkv, "seq", zone, stride, fsdp_count)
    queries = jnp.concatenate([item[:, :part_width] for item in arrived], axis=0)
    pairs = [item[:, part_width:] for item in arrived]
    pairs = jnp.concatenate(
        [item if r == 0 else swap(item, "seq", r) for r in range(stride) for item in pairs], axis=0
    )
    keys, values = pairs[:, :part_width], pairs[:, part_width:]
    source = jnp.stack(
        [((zone ^ m) * stride + (lane ^ r)) for r in range(stride) for m in range(fsdp_count)]
    )
    block_at = jnp.sum(
        jnp.where(
            source[:, None] == jnp.arange(seq_count, dtype=jnp.int32)[None, :], block_order[None, :], 0
        ),
        axis=1,
    )
    position = (
        block_at[:, None] * block_len + jnp.arange(block_len, dtype=jnp.int32)[None, :]
    ).reshape(1, -1)
    bias = jnp.where(position < length, 0.0, masked_out).astype(f32)
    context, lse = attend(queries, keys, values, bias, heads_own)

    up_own = reorder(jnp.stack(columns(up_weight, 1)), me_f).reshape(model_width, -1)

    def home(stack):
        got = [stack[0]] + [swap(stack[m], "seq", m * stride) for m in range(1, fsdp_count)]
        return reorder(jnp.stack(got), zone).reshape(fsdp_count * block_len, -1)

    context_tok = home(context.reshape(fsdp_count, block_len, part_width))
    attended = scatter_rows(dot(context_tok, out_weight), "fsdp") + bias_out
    first_sum = flat_in.astype(f32) + attended
    first_out, first_norm, first_spread = norm_forward(first_sum, gain_one, shift_one)
    first_all = gather_rows(first_out.astype(bf16), "fsdp")
    pre_act = dot(first_all, up_own) + up_bias.astype(f32)
    activated = gelu_exact(pre_act).astype(bf16)
    second_sum = first_out + scatter_rows(dot(activated, down_weight), "fsdp") + bias_down
    second_out, second_norm, second_spread = norm_forward(second_sum, gain_two, shift_two)
    encoded = second_out.astype(bf16).reshape(tokens.shape)
    upstream = cotangent.reshape(block_len, model_width).astype(f32)
    grad_second, grad_gain_two, grad_shift_two = norm_backward(
        upstream, second_norm, second_spread, gain_two
    )
    second_all = gather_rows(grad_second.astype(bf16), "fsdp")
    grad_act = dot_nt(second_all, down_weight)
    grad_pre = grad_act * gelu_slope(pre_act)
    grad_pre_bf = grad_pre.astype(bf16)
    grad_first_out = grad_second + scatter_rows(dot_nt(grad_pre_bf, up_own), "fsdp")
    grad_down = (dot_tn(activated, second_all) * grad_scale).astype(bf16)
    grad_up = (dot_tn(first_all, grad_pre_bf) * grad_scale).astype(bf16)
    grad_first, grad_gain_one, grad_shift_one = norm_backward(
        grad_first_out, first_norm, first_spread, gain_one
    )
    grad_first_all = gather_rows(grad_first.astype(bf16), "fsdp")
    grad_context = dot_nt(grad_first_all, out_weight).astype(bf16)
    grad_out = (dot_tn(context_tok, grad_first_all) * grad_scale).astype(bf16)
    grad_up_rows = jnp.stack(
        exchange(grad_up.reshape(fsdp_count, part_width, -1), "fsdp", me_f, 1, fsdp_count)
    )
    sum_down, sum_up, sum_out = lax.psum((grad_down, grad_up_rows, grad_out), "seq")

    grad_ctx = jnp.concatenate(
        exchange(grad_context.reshape(fsdp_count, block_len, part_width), "seq", zone, stride, fsdp_count),
        axis=0,
    )
    dq, dk, dv = attend_back(queries, keys, values, bias, lse, context, grad_ctx, heads_own)
    rows = fsdp_count * block_len
    dkv = jnp.concatenate([dk, dv], axis=1)
    dkv_own = dkv[:rows]
    for r in range(1, stride):
        dkv_own = dkv_own + swap(dkv[r * rows : (r + 1) * rows].astype(bf16), "seq", r).astype(f32)
    bias_terms = jnp.stack([jnp.sum(dq, axis=0), jnp.sum(dkv_own[:, part_width:], axis=0)])
    dqkv = jnp.concatenate([dq, dkv_own], axis=1).astype(bf16)
    grad_qkv_tok = home(dqkv.reshape(fsdp_count, block_len, 3 * part_width))
    input_grad = grad_first + scatter_rows(dot_nt(grad_qkv_tok, qkv_own), "fsdp")
    grad_qkv = (dot_tn(all_in, grad_qkv_tok) * grad_scale).astype(bf16)

    chunk = part_width // seq_count
    grad_qkv = grad_qkv.reshape(fsdp_count, seq_count, chunk, 3 * part_width)
    piece = halve_sum(jnp.moveaxis(grad_qkv, 1, 0), "seq")
    piece = jnp.stack(exchange(piece, "fsdp", me_f, 1, fsdp_count))
    sum_qkv = double_gather(reorder(piece, me_f), "seq")
    sum_qkv = sum_qkv.reshape(seq_count, fsdp_count, chunk, 3, part_width)
    sum_qkv = sum_qkv.transpose(0, 2, 3, 1, 4).reshape(part_width, 3 * model_width)

    small_all = sum_small(
        jnp.stack(
            [
                jnp.sum(grad_first, axis=0),
                grad_gain_one,
                grad_shift_one,
                jnp.sum(grad_second, axis=0),
                grad_gain_two,
                grad_shift_two,
            ]
        ),
        ("fsdp", "seq"),
    )
    small_own = lax.dynamic_slice_in_dim(small_all, me_f * part_width, part_width, 1) * grad_scale
    bias_sum = sum_small(bias_terms, ("seq",)) * grad_scale
    up_bias_sum = sum_small(jnp.sum(grad_pre, axis=0), ("seq",)) * grad_scale
    up_rows = jnp.moveaxis(reorder(sum_up, me_f), 0, 1).reshape(part_width, -1)

    return (
        encoded,
        input_grad.reshape(tokens.shape),
        sum_qkv.astype(f32),
        bias_sum[0],
        bias_sum[1],
        sum_out.astype(f32),
        small_own[0],
        small_own[1],
        small_own[2],
        up_rows.astype(f32),
        up_bias_sum,
        sum_down.astype(f32),
        small_own[3],
        small_own[4],
        small_own[5],
    )


def solution(mesh):
    rows = P("fsdp", "seq", None)
    matrix = P("fsdp", None)
    vector = P("fsdp")
    return jax.shard_map(
        body,
        mesh=mesh,
        in_specs=(
            rows,
            vector,
            P(),
            matrix,
            vector,
            vector,
            matrix,
            vector,
            vector,
            vector,
            matrix,
            vector,
            matrix,
            vector,
            vector,
            vector,
            rows,
        ),
        out_specs=(
            rows,
            rows,
            matrix,
            vector,
            vector,
            matrix,
            vector,
            vector,
            vector,
            matrix,
            vector,
            matrix,
            vector,
            vector,
            vector,
        ),
        check_vma=False,
    )
```

```python
import functools

import jax
import jax.numpy as jnp
from jax import lax
from jax.experimental import pallas as pl
from jax.experimental.pallas import tpu as pltpu
from jax.sharding import PartitionSpec as P


HEADS = 12

epsilon = 1e-06
masked_out = -1e30
bf16 = jnp.bfloat16
f32 = jnp.float32


def norm_forward(hidden, gain, shift):
    centre = hidden - jnp.mean(hidden, axis=-1, keepdims=True)
    spread = lax.rsqrt(jnp.mean(centre * centre, axis=-1, keepdims=True) + epsilon)
    normed = centre * spread
    return (normed * gain + shift, normed, spread)


def norm_backward(upstream, normed, spread, gain):
    scaled = upstream * gain
    grad_in = spread * (
        scaled
        - jnp.mean(scaled, axis=-1, keepdims=True)
        - normed * jnp.mean(scaled * normed, axis=-1, keepdims=True)
    )
    return (grad_in, jnp.sum(upstream * normed, axis=0), jnp.sum(upstream, axis=0))


def swap(value, axis, mask):
    count = lax.axis_size(axis)
    return lax.ppermute(value, axis, [(i, i ^ mask) for i in range(count)])


def masks_of(count):
    found = []
    bit = 1
    while bit < count:
        found.append(bit)
        bit *= 2
    return found


def pick(stack, index, axis=0):
    return lax.dynamic_index_in_dim(stack, index, axis, keepdims=False)


def join_kernel(me_ref, *refs):
    *in_refs, out_ref = refs
    rows = in_refs[0].shape[0]
    for m, in_ref in enumerate(in_refs):
        start = pl.multiple_of(lax.bitwise_xor(me_ref[0], m) * rows, rows)
        out_ref[pl.ds(start, rows), :] = in_ref[...]


def join_rows(parts, me):
    rows, width = parts[0].shape
    vmem = pl.BlockSpec(memory_space=pltpu.VMEM)
    return pl.pallas_call(
        join_kernel,
        in_specs=[pl.BlockSpec(memory_space=pltpu.SMEM)] + [vmem] * len(parts),
        out_specs=vmem,
        out_shape=jax.ShapeDtypeStruct((len(parts) * rows, width), parts[0].dtype),
        name="join_rows",
    )(me, *parts)


def attend_kernel(heads, size, scale, q_ref, k_ref, v_ref, bias_ref, ctx_ref, lse_ref):
    bias = bias_ref[...]
    lanes = lax.broadcasted_iota(jnp.int32, lse_ref.shape, 1)
    stats = jnp.zeros(lse_ref.shape, f32)
    outs = []
    for h in range(heads):
        cols = slice(h * size, (h + 1) * size)
        logits = (
            lax.dot_general(
                q_ref[:, cols], k_ref[:, cols], (((1,), (1,)), ((), ())), preferred_element_type=f32
            )
            * scale
            + bias
        )
        top = jnp.max(logits, axis=-1, keepdims=True)
        terms = jnp.exp(logits - top)
        total = jnp.sum(terms, axis=-1, keepdims=True)
        context = jnp.dot(terms.astype(bf16), v_ref[:, cols], preferred_element_type=f32)
        outs.append(context / total)
        stats = jnp.where(lanes == h, top + jnp.log(total), stats)
    ctx_ref[...] = jnp.concatenate(outs, axis=1).astype(bf16)
    lse_ref[...] = stats


def attend(queries, keys, values, bias, heads):
    rows, width = queries.shape
    full_len = keys.shape[0]
    size = width // heads
    tile = min(128, rows)
    whole = lambda i: (0, 0)
    return pl.pallas_call(
        functools.partial(attend_kernel, heads, size, size ** (-0.5)),
        grid=(rows // tile,),
        in_specs=[
            pl.BlockSpec((tile, width), lambda i: (i, 0)),
            pl.BlockSpec((full_len, width), whole),
            pl.BlockSpec((full_len, width), whole),
            pl.BlockSpec((1, full_len), whole),
        ],
        out_specs=[
            pl.BlockSpec((tile, width), lambda i: (i, 0)),
            pl.BlockSpec((tile, 128), lambda i: (i, 0)),
        ],
        out_shape=[
            jax.ShapeDtypeStruct((rows, width), bf16),
            jax.ShapeDtypeStruct((rows, 128), f32),
        ],
        cost_estimate=pl.CostEstimate(
            flops=4 * rows * full_len * width,
            bytes_accessed=4 * (rows + full_len) * width,
            transcendentals=rows * full_len * heads,
        ),
        name="attend",
    )(queries, keys, values, bias)


def attend_back_kernel(
    heads, size, scale, q_ref, k_ref, v_ref, bias_ref, lse_ref, ctx_ref, g_ref, dq_ref, dk_ref, dv_ref
):
    @pl.when(pl.program_id(0) == 0)
    def _():
        dk_ref[...] = jnp.zeros_like(dk_ref)
        dv_ref[...] = jnp.zeros_like(dv_ref)

    bias = bias_ref[...]
    dqs, dks, dvs = [], [], []
    for h in range(heads):
        cols = slice(h * size, (h + 1) * size)
        q_h, k_h, v_h, g_h = q_ref[:, cols], k_ref[:, cols], v_ref[:, cols], g_ref[:, cols]
        logits = (
            lax.dot_general(q_h, k_h, (((1,), (1,)), ((), ())), preferred_element_type=f32) * scale
            + bias
        )
        probs = jnp.exp(logits - lse_ref[:, h : h + 1])
        grad_logit = lax.dot_general(
            g_h, v_h, (((1,), (1,)), ((), ())), preferred_element_type=f32
        )
        correction = jnp.sum(
            g_h.astype(f32) * ctx_ref[:, cols].astype(f32), axis=-1, keepdims=True
        )
        mixed = (probs * (grad_logit - correction)).astype(bf16)
        dqs.append(jnp.dot(mixed, k_h, preferred_element_type=f32) * scale)
        dks.append(
            lax.dot_general(mixed, q_h, (((0,), (0,)), ((), ())), preferred_element_type=f32)
            * scale
        )
        dvs.append(
            lax.dot_general(
                probs.astype(bf16), g_h, (((0,), (0,)), ((), ())), preferred_element_type=f32
            )
        )
    dq_ref[...] = jnp.concatenate(dqs, axis=1)
    dk_ref[...] += jnp.concatenate(dks, axis=1)
    dv_ref[...] += jnp.concatenate(dvs, axis=1)


def attend_back(queries, keys, values, bias, lse, context, grad, heads):
    rows, width = queries.shape
    full_len = keys.shape[0]
    size = width // heads
    tile = min(128, rows)
    whole = lambda i: (0, 0)
    part = lambda i: (i, 0)
    return pl.pallas_call(
        functools.partial(attend_back_kernel, heads, size, size ** (-0.5)),
        grid=(rows // tile,),
        in_specs=[
            pl.BlockSpec((tile, width), part),
            pl.BlockSpec((full_len, width), whole),
            pl.BlockSpec((full_len, width), whole),
            pl.BlockSpec((1, full_len), whole),
            pl.BlockSpec((tile, 128), part),
            pl.BlockSpec((tile, width), part),
            pl.BlockSpec((tile, width), part),
        ],
        out_specs=[
            pl.BlockSpec((tile, width), part),
            pl.BlockSpec((full_len, width), whole),
            pl.BlockSpec((full_len, width), whole),
        ],
        out_shape=[
            jax.ShapeDtypeStruct((rows, width), f32),
            jax.ShapeDtypeStruct((full_len, width), f32),
            jax.ShapeDtypeStruct((full_len, width), f32),
        ],
        cost_estimate=pl.CostEstimate(
            flops=10 * rows * full_len * width,
            bytes_accessed=8 * (rows + full_len) * width,
            transcendentals=rows * full_len * heads,
        ),
        name="attend_back",
    )(queries, keys, values, bias, lse, context, grad)


def dot(a, b):
    return jnp.dot(a, b, preferred_element_type=f32)


def dot_nt(a, b):
    return lax.dot_general(a, b, (((1,), (1,)), ((), ())), preferred_element_type=f32)


def dot_tn(a, b):
    return lax.dot_general(a, b, (((0,), (0,)), ((), ())), preferred_element_type=f32)


def after(value, *others):
    return lax.optimization_barrier((value,) + others)[0]


def halve(value, mask):
    me = lax.axis_index("seq")
    half = value.shape[0] // 2
    low = jnp.where(me & mask == 0, 0, half)
    sent = lax.dynamic_slice_in_dim(value, half - low, half, 0)
    kept = lax.dynamic_slice_in_dim(value, low, half, 0)
    return (kept.astype(f32) + swap(sent, "seq", mask).astype(f32)).astype(bf16)


def double(value, mask):
    first = lax.axis_index("seq") & mask == 0
    other = swap(value, "seq", mask)
    return jnp.concatenate(
        [jnp.where(first, value, other), jnp.where(first, other, value)], axis=0
    )


def reduce_seq(value):
    for mask in masks_of(lax.axis_size("seq")):
        value = halve(value, mask)
    return value


def gather_seq(value):
    for mask in reversed(masks_of(lax.axis_size("seq"))):
        value = double(value, mask)
    return value


def project_kernel(parts, where_ref, *refs):
    in_ref, full_ref = refs[:2]
    weights, outs = refs[2 : 2 + parts], refs[2 + parts : 2 + 2 * parts]
    in4, out4 = refs[2 + 2 * parts :]
    me, zone = where_ref[0], where_ref[1]
    width = in4.shape[2]
    for g in range(parts):
        in4[g] = in_ref[:, g * width : (g + 1) * width]
    total = dot(in4[me], weights[0][...])
    for m in range(1, parts):
        total += dot(in4[lax.bitwise_xor(me, m)], weights[m][...])
    rows = total.shape[1] // 3
    queries = (total[:, :rows] + full_ref[6:7, :]).astype(bf16)
    keys = total[:, rows : 2 * rows].astype(bf16)
    values = (total[:, 2 * rows :] + full_ref[7:8, :]).astype(bf16)
    for g in range(parts):
        cols = slice(g * width, (g + 1) * width)
        out4[g] = jnp.concatenate([queries[:, cols], keys[:, cols], values[:, cols]], axis=1)
    for m in range(parts):
        outs[m][...] = out4[lax.bitwise_xor(zone, m)]


def project(where, flat_in, full, weights):
    parts = len(weights)
    rows, width = flat_in.shape
    share = width // parts
    vmem = pl.BlockSpec(memory_space=pltpu.VMEM)
    return pl.pallas_call(
        functools.partial(project_kernel, parts),
        in_specs=[pl.BlockSpec(memory_space=pltpu.SMEM)] + [vmem] * (parts + 2),
        out_specs=[vmem] * parts,
        out_shape=[jax.ShapeDtypeStruct((rows, 3 * share), bf16)] * parts,
        scratch_shapes=[
            pltpu.VMEM((parts, rows, share), bf16),
            pltpu.VMEM((parts, rows, 3 * share), bf16),
        ],
        name="project",
    )(where, flat_in, full, *weights)


def mix_kernel(parts, where_ref, *refs):
    got, out_ref = refs[:parts], refs[parts]
    width = got[0].shape[1] // 3
    for m in range(parts):
        for g in range(parts):

            @pl.when(lax.bitwise_xor(where_ref[1], m) == g)
            def _():
                for p in range(3):
                    start = (p * parts + g) * width
                    out_ref[:, start : start + width] = got[m][:, p * width : (p + 1) * width]


def mix_heads(where, got):
    parts = len(got)
    rows, width = got[0].shape
    vmem = pl.BlockSpec(memory_space=pltpu.VMEM)
    return pl.pallas_call(
        functools.partial(mix_kernel, parts),
        in_specs=[pl.BlockSpec(memory_space=pltpu.SMEM)] + [vmem] * parts,
        out_specs=vmem,
        out_shape=jax.ShapeDtypeStruct((rows, parts * width), bf16),
        name="mix_heads",
    )(where, *got)


def middle_kernel(parts, where_ref, *refs):
    refs = list(refs)

    def take(count):
        found = refs[:count]
        del refs[:count]
        return found

    got, out_w, up_w, down_w = take(parts), take(parts), take(parts), take(parts)
    in_ref, full_ref, bias_up_ref, cot_ref = take(4)
    enc_ref, grad_first_ref, first_bf_ref, grad_pre_ref, second_bf_ref, grad_first_bf_ref = take(6)
    sums_ref, up_sums_ref = take(2)
    act_out, first_out_refs, ctx_out, grad_out = take(parts), take(parts), take(parts), take(parts)
    ctx4, first4, act4, slope4, pre4, add4, grad4 = take(7)
    me, zone = where_ref[0], where_ref[1]
    at = [lax.bitwise_xor(me, m) for m in range(parts)]
    width = first4.shape[2]
    ff_width = act4.shape[2]

    def row(i):
        return full_ref[i : i + 1, :]

    for m in range(parts):
        ctx4[lax.bitwise_xor(zone, m)] = got[m][...]
    attended = dot(ctx4[at[0]], out_w[0][...])
    for m in range(1, parts):
        attended += dot(ctx4[at[m]], out_w[m][...])
    first, first_norm, first_spread = norm_forward(
        in_ref[...].astype(f32) + attended + row(0), row(1), row(2)
    )
    first_bf = first.astype(bf16)
    first_bf_ref[...] = first_bf
    for g in range(parts):
        first4[g] = first_bf[:, g * width : (g + 1) * width]

    def up_step(c, _):
        cols = pl.ds(pl.multiple_of(c * ff_width, ff_width), ff_width)
        pre = dot(first4[at[0]], up_w[0][:, cols])
        for m in range(1, parts):
            pre += dot(first4[at[m]], up_w[m][:, cols])
        pre += bias_up_ref[:, cols]
        share = 0.5 * (1.0 + lax.erf(pre * 0.7071067811865476))
        act4[c] = (pre * share).astype(bf16)
        slope4[c] = share + pre * jnp.exp(-0.5 * pre * pre) * 0.3989422804014327
        return 0

    lax.fori_loop(0, parts, up_step, 0)
    second = first + row(3)
    for m in range(parts):
        second += dot(act4[at[m]], down_w[m][...])
    encoded, second_norm, second_spread = norm_forward(second, row(4), row(5))
    enc_ref[...] = encoded.astype(bf16)
    upstream = cot_ref[...].astype(f32)
    grad_second, gain_two, shift_two = norm_backward(upstream, second_norm, second_spread, row(4))
    grad_second_bf = grad_second.astype(bf16)
    second_bf_ref[...] = grad_second_bf
    for m in range(parts):
        grad = dot_nt(grad_second_bf, down_w[m][...]) * slope4[at[m]]
        up_sums_ref[pl.ds(at[m], 1), :] = jnp.sum(grad, axis=0, keepdims=True)
        pre4[at[m]] = grad.astype(bf16)
    for m in range(parts):
        total = dot_nt(pre4[0], up_w[m][:, :ff_width])
        for c in range(1, parts):
            total += dot_nt(pre4[c], up_w[m][:, c * ff_width : (c + 1) * ff_width])
        add4[at[m]] = total
    grad_first_out = grad_second + jnp.concatenate([add4[g] for g in range(parts)], axis=1)
    grad_first, gain_one, shift_one = norm_backward(
        grad_first_out, first_norm, first_spread, row(1)
    )
    grad_first_ref[...] = grad_first
    grad_first_bf = grad_first.astype(bf16)
    grad_first_bf_ref[...] = grad_first_bf
    for m in range(parts):
        grad4[at[m]] = dot_nt(grad_first_bf, out_w[m][...]).astype(bf16)
    for m in range(parts):
        grad_pre_ref[:, m * ff_width : (m + 1) * ff_width] = pre4[m]
        act_out[m][...] = act4[at[m]]
        first_out_refs[m][...] = first4[at[m]]
        ctx_out[m][...] = ctx4[at[m]]
        grad_out[m][...] = grad4[lax.bitwise_xor(zone, m)]
    lines = [
        jnp.sum(grad_first, axis=0),
        gain_one,
        shift_one,
        jnp.sum(grad_second, axis=0),
        gain_two,
        shift_two,
    ]
    for i, line in enumerate(lines):
        sums_ref[i : i + 1, :] = line[None]
    sums_ref[len(lines) :, :] = jnp.zeros((sums_ref.shape[0] - len(lines), line.shape[0]), f32)


def middle(where, got, out_w, up_w, down_w, flat_in, full, bias_up, cot):
    parts = len(got)
    rows, width = flat_in.shape
    share, ff_width = width // parts, bias_up.shape[1] // parts
    vmem = pl.BlockSpec(memory_space=pltpu.VMEM)
    shape = jax.ShapeDtypeStruct
    outs = [
        shape((rows, width), bf16),
        shape((rows, width), f32),
        shape((rows, width), bf16),
        shape((rows, bias_up.shape[1]), bf16),
        shape((rows, width), bf16),
        shape((rows, width), bf16),
        shape((8, width), f32),
        shape((parts, ff_width), f32),
    ]
    outs += [shape((rows, ff_width), bf16)] * parts + [shape((rows, share), bf16)] * (3 * parts)
    weights = (2 * width + 4 * bias_up.shape[1]) * width
    found = pl.pallas_call(
        functools.partial(middle_kernel, parts),
        in_specs=[pl.BlockSpec(memory_space=pltpu.SMEM)] + [vmem] * (4 * parts + 4),
        out_specs=[vmem] * len(outs),
        out_shape=outs,
        scratch_shapes=[
            pltpu.VMEM((parts, rows, share), bf16),
            pltpu.VMEM((parts, rows, share), bf16),
            pltpu.VMEM((parts, rows, ff_width), bf16),
            pltpu.VMEM((parts, rows, ff_width), f32),
            pltpu.VMEM((parts, rows, ff_width), bf16),
            pltpu.VMEM((parts, rows, share), f32),
            pltpu.VMEM((parts, rows, share), bf16),
        ],
        cost_estimate=pl.CostEstimate(
            flops=2 * rows * weights, bytes_accessed=2 * weights, transcendentals=3 * rows * bias_up.shape[1]
        ),
        name="middle",
    )(where, *got, *out_w, *up_w, *down_w, flat_in, full, bias_up, cot)
    head, tail = found[:8], found[8:]
    return head, [list(tail[i * parts : (i + 1) * parts]) for i in range(4)]


def pack_kernel(*refs):
    *in_refs, out_ref = refs
    width = out_ref.shape[1]
    row = 0
    for ref in in_refs:
        line = ref[...].astype(f32)
        for i in range(0, line.shape[0], width):
            out_ref[row, :] = line[i : i + width]
            row += 1
    for i in range(row, out_ref.shape[0]):
        out_ref[i, :] = jnp.zeros((width,), f32)


def pack_rows(vectors, width):
    count = sum(item.shape[0] // width for item in vectors)
    return pl.pallas_call(
        pack_kernel,
        out_shape=jax.ShapeDtypeStruct((count + 8 - count % 8, width), f32),
        name="pack_rows",
    )(*vectors)


def unpack_kernel(short, me_ref, *refs):
    *in_refs, full_ref, long_ref = refs
    width = in_refs[0].shape[1]
    pieces = long_ref.shape[1] // (width * len(in_refs))
    for m, in_ref in enumerate(in_refs):
        for g in range(len(in_refs)):

            @pl.when(lax.bitwise_xor(me_ref[0], m) == g)
            def _():
                full_ref[:, g * width : (g + 1) * width] = in_ref[:short, :]
                for i in range(pieces):
                    start = (g * pieces + i) * width
                    long_ref[:, start : start + width] = in_ref[short + i : short + i + 1, :]


def unpack_rows(parts, me, short, pieces):
    width = parts[0].shape[1] * len(parts)
    vmem = pl.BlockSpec(memory_space=pltpu.VMEM)
    return pl.pallas_call(
        functools.partial(unpack_kernel, short),
        in_specs=[pl.BlockSpec(memory_space=pltpu.SMEM)] + [vmem] * len(parts),
        out_specs=[vmem] * 2,
        out_shape=[
            jax.ShapeDtypeStruct((short, width), f32),
            jax.ShapeDtypeStruct((1, width * pieces), f32),
        ],
        name="unpack_rows",
    )(me, *parts)


def after(value, *others):
    return lax.optimization_barrier((value,) + others)[0]


def halve(value, mask):
    me = lax.axis_index("seq")
    half = value.shape[0] // 2
    low = jnp.where(me & mask == 0, 0, half)
    sent = lax.dynamic_slice_in_dim(value, half - low, half, 0)
    kept = lax.dynamic_slice_in_dim(value, low, half, 0)
    return (kept.astype(f32) + swap(sent, "seq", mask).astype(f32)).astype(bf16)


def double(value, mask):
    first = lax.axis_index("seq") & mask == 0
    other = swap(value, "seq", mask)
    return jnp.concatenate(
        [jnp.where(first, value, other), jnp.where(first, other, value)], axis=0
    )


def pack_kernel(*refs):
    *in_refs, out_ref = refs
    width = out_ref.shape[1]
    row = 0
    for ref in in_refs:
        line = ref[...].astype(f32)
        for i in range(0, line.shape[0], width):
            out_ref[row, :] = line[i : i + width]
            row += 1
    for i in range(row, out_ref.shape[0]):
        out_ref[i, :] = jnp.zeros((width,), f32)


def pack_rows(vectors, width):
    count = sum(item.shape[0] // width for item in vectors)
    return pl.pallas_call(
        pack_kernel,
        out_shape=jax.ShapeDtypeStruct((count + 8 - count % 8, width), f32),
        name="pack_rows",
    )(*vectors)


def unpack_kernel(short, me_ref, *refs):
    *in_refs, full_ref, long_ref = refs
    width = in_refs[0].shape[1]
    pieces = long_ref.shape[1] // (width * len(in_refs))
    for m, in_ref in enumerate(in_refs):
        for g in range(len(in_refs)):

            @pl.when(lax.bitwise_xor(me_ref[0], m) == g)
            def _():
                full_ref[:, g * width : (g + 1) * width] = in_ref[:short, :]
                for i in range(pieces):
                    start = (g * pieces + i) * width
                    long_ref[:, start : start + width] = in_ref[short + i : short + i + 1, :]


def unpack_rows(parts, me, short, pieces):
    width = parts[0].shape[1] * len(parts)
    vmem = pl.BlockSpec(memory_space=pltpu.VMEM)
    return pl.pallas_call(
        functools.partial(unpack_kernel, short),
        in_specs=[pl.BlockSpec(memory_space=pltpu.SMEM)] + [vmem] * len(parts),
        out_specs=[vmem] * 2,
        out_shape=[
            jax.ShapeDtypeStruct((short, width), f32),
            jax.ShapeDtypeStruct((1, width * pieces), f32),
        ],
        name="unpack_rows",
    )(me, *parts)


def body(
    tokens,
    lengths,
    block_order,
    qkv_weight,
    q_bias,
    v_bias,
    out_weight,
    out_bias,
    norm1_gain,
    norm1_shift,
    up_weight,
    up_bias,
    down_weight,
    down_bias,
    norm2_gain,
    norm2_shift,
    cotangent,
):
    seq_local, block_len, model_width = tokens.shape
    seq_count = lax.axis_size("seq")
    fsdp_count = lax.axis_size("fsdp")
    me_f = lax.axis_index("fsdp")
    me_s = lax.axis_index("seq")
    me = me_f.astype(jnp.int32).reshape(1)
    zones = fsdp_count
    stride = seq_count // zones
    zone = me_s // stride
    lane = me_s % stride
    part_width = model_width // fsdp_count
    heads_own = HEADS // fsdp_count
    grad_scale = (block_len * seq_local * seq_count * fsdp_count) ** (-0.5)
    fsdp_masks = masks_of(fsdp_count)

    def weight_parts(weight):
        parts = {0: weight}
        for mask in reversed(fsdp_masks):
            for m in list(parts):
                parts[m ^ mask] = swap(parts[m], "fsdp", mask)
        return [parts[m] for m in range(fsdp_count)]

    flat_in = tokens.reshape(block_len, model_width)
    qkv_parts = weight_parts(qkv_weight)
    out_parts = weight_parts(out_weight)
    up_parts = weight_parts(up_weight)
    down_parts = weight_parts(down_weight)

    up_rows = up_bias.shape[0] // part_width
    packed = pack_rows(
        [out_bias, norm1_gain, norm1_shift, down_bias, norm2_gain, norm2_shift, q_bias, v_bias, up_bias],
        part_width,
    )
    full, bias_up = unpack_rows(weight_parts(packed), me, 8, up_rows)

    where = jnp.stack([me_f, zone]).astype(jnp.int32)
    qkv = project(where, flat_in, full, qkv_parts)
    arrived = [qkv[0]] + [swap(qkv[m], "seq", m * stride) for m in range(1, zones)]
    queries = jnp.concatenate([item[:, :part_width] for item in arrived], axis=0)
    pairs = jnp.concatenate([item[:, part_width:] for item in arrived], axis=0)
    pairs = jnp.concatenate(
        [pairs if r == 0 else swap(pairs, "seq", r) for r in range(stride)], axis=0
    )
    keys, values = pairs[:, :part_width], pairs[:, part_width:]
    source = jnp.stack(
        [((zone ^ m) * stride + (lane ^ r)) for r in range(stride) for m in range(zones)]
    )
    block_at = jnp.sum(
        jnp.where(
            source[:, None] == jnp.arange(seq_count, dtype=jnp.int32)[None, :], block_order[None, :], 0
        ),
        axis=1,
    )
    position = (
        block_at[:, None] * block_len + jnp.arange(block_len, dtype=jnp.int32)[None, :]
    ).reshape(1, -1)
    bias = jnp.where(position < lengths[0], 0.0, masked_out).astype(f32)
    context, lse = attend(queries, keys, values, bias, heads_own)

    def home(stack):
        return [stack[0]] + [swap(stack[m], "seq", m * stride) for m in range(1, zones)]

    got = home(context.reshape(zones, block_len, part_width))
    (
        (encoded, grad_first, first_bf, grad_pre_bf, grad_second_bf, grad_first_bf, sums_own, up_sums),
        (act_blocks, first_blocks, ctx_blocks, grad_blocks),
    ) = middle(
        where,
        got,
        out_parts,
        up_parts,
        down_parts,
        flat_in,
        full,
        bias_up,
        cotangent.reshape(block_len, model_width),
    )
    encoded = encoded.reshape(tokens.shape)

    def hop(state, mask):
        blocks, shared = state
        width = blocks[0].shape[1]
        sent = blocks[mask] if mask == 1 else jnp.concatenate(blocks[mask:], axis=1)
        other = swap(shared, "fsdp", mask)
        got = swap(sent, "fsdp", mask)
        kept = [
            jnp.concatenate([blocks[r], got[:, r * width : (r + 1) * width]], axis=0)
            for r in range(mask)
        ]
        return kept, jnp.concatenate([shared, other], axis=0)

    def send(blocks, shared):
        state = blocks, shared
        for mask in reversed(fsdp_masks[1:]):
            state = hop(state, mask)
        return state

    def finish(state, *others):
        blocks, shared = hop(after(state, *others), 1)
        return blocks[0], shared

    def split(value):
        return jnp.moveaxis(value.reshape(block_len, fsdp_count, -1), 1, 0)

    def relative(stack):
        return [pick(stack, me_f ^ r) for r in range(fsdp_count)]

    def weight_term(left, right):
        return (dot_tn(left, right) * grad_scale).astype(bf16)

    ff = up_bias.shape[0] * fsdp_count
    in_blocks = relative(split(flat_in))
    out_blocks = [
        jnp.concatenate([a, b], axis=1) for a, b in zip(ctx_blocks, in_blocks)
    ]
    down_sent = send(act_blocks, grad_second_bf)
    up_sent = send(first_blocks, grad_pre_bf)
    out_sent = send(out_blocks, grad_first_bf)

    grad_ctx = jnp.concatenate(
        [grad_blocks[0]]
        + [swap(grad_blocks[m], "seq", m * stride) for m in range(1, zones)],
        axis=0,
    )
    dq, dk, dv = attend_back(queries, keys, values, bias, lse, context, grad_ctx, heads_own)
    grad_down = weight_term(*finish(down_sent, dq))
    rows = zones * block_len
    dkv = jnp.concatenate([dk, dv], axis=1)
    dkv_own = dkv[:rows]
    others = [swap(dkv[r * rows : (r + 1) * rows].astype(bf16), "seq", r) for r in range(1, stride)]
    for item in others:
        dkv_own = dkv_own + item.astype(f32)
    bias_terms = jnp.stack([jnp.sum(dq, axis=0), jnp.sum(dkv_own[:, part_width:], axis=0)])
    dqkv = jnp.concatenate([dq, dkv_own], axis=1).astype(bf16)
    grad_qkv_tok = home(dqkv.reshape(zones, block_len, 3 * part_width))
    grad_qkv_tok = mix_heads(where, grad_qkv_tok)
    qkv_full = join_rows(qkv_parts, me)
    input_grad = grad_first + dot_nt(grad_qkv_tok, qkv_full)
    qkv_sent = grad_qkv_tok
    for mask in reversed(fsdp_masks[1:]):
        qkv_sent = jnp.concatenate([qkv_sent, swap(qkv_sent, "fsdp", mask)], axis=0)
    grad_up = weight_term(*finish(up_sent, grad_qkv_tok))
    out_own, first_grads = finish(out_sent, qkv_sent)
    grad_out = weight_term(out_own[:, :part_width], first_grads)
    in_own = out_own[:, part_width:]
    grad_uo = jnp.concatenate([grad_up, grad_out], axis=1)
    qkv_sent = jnp.concatenate([qkv_sent, swap(qkv_sent, "fsdp", 1)], axis=0)
    grad_qkv = weight_term(in_own, qkv_sent)
    shares = [reduce_seq(item) for item in (grad_down, grad_uo, grad_qkv)]
    sum_down = gather_seq(shares[0])
    sum_uo = gather_seq(shares[1])
    sum_qkv = gather_seq(shares[2])
    sum_up, sum_out = sum_uo[:, :ff], sum_uo[:, ff:]

    terms = sums_own[:6].reshape(6, fsdp_count, part_width)
    heads = jnp.arange(zones)[:, None, None]
    terms = jnp.concatenate(
        [
            jnp.moveaxis(terms, 1, 0),
            up_sums.reshape(fsdp_count, up_rows, part_width),
            jnp.where(heads == zone, bias_terms[None], 0.0),
        ],
        axis=1,
    )
    for mask in fsdp_masks:
        terms = terms + swap(terms, "fsdp", mask)
    sums = pick(terms, me_f)
    for mask in masks_of(seq_count):
        sums = sums + swap(sums, "seq", mask)
    sums = sums * grad_scale

    return (
        encoded,
        input_grad.reshape(tokens.shape),
        sum_qkv.astype(f32),
        sums[-2],
        sums[-1],
        sum_out.astype(f32),
        sums[0],
        sums[1],
        sums[2],
        sum_up.astype(f32),
        sums[6:-2].reshape(up_bias.shape),
        sum_down.astype(f32),
        sums[3],
        sums[4],
        sums[5],
    )


def solution(mesh):
    rows = P("fsdp", "seq", None)
    matrix = P("fsdp", None)
    vector = P("fsdp")

    return jax.shard_map(
        body,
        mesh=mesh,
        in_specs=(
            rows,
            vector,
            P(),
            matrix,
            vector,
            vector,
            matrix,
            vector,
            vector,
            vector,
            matrix,
            vector,
            matrix,
            vector,
            vector,
            vector,
            rows,
        ),
        out_specs=(
            rows,
            rows,
            matrix,
            vector,
            vector,
            matrix,
            vector,
            vector,
            vector,
            matrix,
            vector,
            matrix,
            vector,
            vector,
            vector,
        ),
        check_vma=False,
    )
```
